32 devices in a mesh: blk: 4 (over x, core), inner: 8 (over z, y).
Axes of the slice: x: 2, y: 2, z: 4, core: 2. Of those that a mesh axis runs over, the one named last changes fastest.
Arguments:
- queries: bfloat16 [4096, 1024], P(('blk', 'inner')), may hold values from -9 to 9
- keys: bfloat16 [4096, 128], P(('blk', 'inner')), may hold values from -4 to 4
- values: bfloat16 [4096, 128], P(('blk', 'inner')), may hold values from -6 to 6
- out_grad: bfloat16 [4096, 1024], P(('blk', 'inner')), may hold values from -6 to 6
- block_list: int32 [32, 5], P(('blk', 'inner')), may hold values from 0 to 31, as said below
Outputs:
- attended: bfloat16 [4096, 1024], P(('blk', 'inner'))
- grad_queries: bfloat16 [4096, 1024], P(('blk', 'inner'))
- grad_keys: float32 [4096, 128], P(('blk', 'inner'))
- grad_values: float32 [4096, 128], P(('blk', 'inner'))
The draws below stay inside these ranges and needn't reach their ends.
Inputs may be any that keep to these rules, and one draw needn't show every extreme that they name: `block_list`: for query block q, entry n < 2 is max(q - min(n, w - 1), 0) with one w of 2 to 2 a row; each entry n >= 2 is a * 8 for some a with a * 8 <= q.
All inputs are finite; a program needn't handle non-finite values.
Results may differ from the reference program's by a relative error of at most 0.0095.
Values may be sent and summed in bfloat16 or wider, within the bound.
A program may use at most 64 MiB of HBM per device.

```python
import jax
import jax.numpy as jnp
from jax import lax

HEADS = 8
HEAD_DIM = 128
BLOCK = 128
STRIPES = 3
BAND = 2
NB = 5
TOKENS = 4096
QBLOCKS = 32
GROUP_BLOCKS = 8


def draw_keys(key, part):
    base = jax.random.truncated_normal(jax.random.fold_in(key, 1), -4.0, 4.0, (TOKENS, HEAD_DIM), jnp.float32)
    return base.astype(jnp.bfloat16)


def draw_queries(key, part):
    base = jax.random.truncated_normal(jax.random.fold_in(key, 11), -4.0, 4.0, (TOKENS, HEADS * HEAD_DIM), jnp.float32)
    return base.astype(jnp.bfloat16)


def draw_block_list(key, part):
    block_numbers = jnp.arange(QBLOCKS, dtype=jnp.int32)
    band_width = jax.random.randint(jax.random.fold_in(key, 21), (QBLOCKS, 1), 2, BAND + 1)
    offsets = jnp.minimum(jnp.arange(BAND, dtype=jnp.int32)[None, :], band_width - 1)
    band = jnp.maximum(block_numbers[:, None] - offsets, 0)
    group_ids = block_numbers // GROUP_BLOCKS
    anchor_block = jax.random.randint(jax.random.fold_in(key, 22), (QBLOCKS, STRIPES), 0, group_ids[:, None] + 1)
    return jnp.concatenate([band, anchor_block * GROUP_BLOCKS], axis=1).astype(jnp.int32)


def levels(stream_key, shape, split, low, high):
    factor_of = 1.0
    for dim, parts in split:
        draws = jax.random.uniform(jax.random.fold_in(jax.random.fold_in(stream_key, 6), dim), (parts,), jnp.float32, low / len(split), high / len(split))
        factor_of = factor_of * jnp.repeat(jnp.exp(draws), shape[dim] // parts).reshape((-1,) + (1,) * (len(shape) - 1 - dim))
    return factor_of


def bell_draw(rng, shape, width, bound, split=(), kind=jnp.bfloat16):
    entries = width * jax.random.normal(rng, shape, jnp.float32)
    if split:
        entries = entries * levels(rng, shape, split, -0.22, 0.18)
    return jnp.clip(entries, -bound, bound).astype(kind)


def setup_inputs(seed: int = 0) -> dict:
    key_list = jax.random.split(jax.random.key(seed), 6)
    return {
        "queries": draw_queries(jax.random.fold_in(key_list[5], 71), 0),
        "keys": draw_keys(jax.random.fold_in(key_list[5], 71), 0),
        "values": bell_draw(key_list[2], (TOKENS, HEAD_DIM), 1.0, 6.0, ((0, 32),)),
        "out_grad": bell_draw(key_list[3], (TOKENS, HEADS * HEAD_DIM), 1.0, 6.0, ((0, 32),)),
        "block_list": draw_block_list(jax.random.fold_in(key_list[5], 71), 0),
    }


NEG = -1e30


def reference(queries, keys, values, out_grad, block_list):
    scale = HEAD_DIM ** -0.5
    key_blocks = keys.reshape(QBLOCKS, BLOCK, HEAD_DIM)
    value_blocks = values.reshape(QBLOCKS, BLOCK, HEAD_DIM)
    query_blocks = queries.reshape(QBLOCKS, BLOCK, HEADS, HEAD_DIM)
    grad_blocks = out_grad.reshape(QBLOCKS, BLOCK, HEADS, HEAD_DIM)

    def one_block(block_id):
        row = block_list[block_id]
        band_ids = block_id - BAND + 1 + jnp.arange(BAND, dtype=jnp.int32)
        band_live = (band_ids >= 0) & jnp.any(row[None, :] == band_ids[:, None], axis=1)
        stripe_ids = row[BAND:]
        order = jnp.arange(STRIPES, dtype=jnp.int32)
        repeated = jnp.any((stripe_ids[:, None] == stripe_ids[None, :]) & (order[None, :] < order[:, None]), axis=1)
        in_band = jnp.any((stripe_ids[:, None] == band_ids[None, :]) & band_live[None, :], axis=1)
        stripe_live = jnp.logical_not(in_band) & jnp.logical_not(repeated)
        entry_ids = jnp.concatenate([jnp.maximum(band_ids, 0), stripe_ids]).astype(jnp.int32)
        entry_live = jnp.concatenate([band_live, stripe_live])
        key_matrix_rows = key_blocks[entry_ids].reshape(NB * BLOCK, HEAD_DIM).astype(jnp.float32)
        value_matrix_rows = value_blocks[entry_ids].reshape(NB * BLOCK, HEAD_DIM).astype(jnp.float32)
        key_tokens = (entry_ids[:, None] * BLOCK + jnp.arange(BLOCK, dtype=jnp.int32)[None, :]).reshape(-1)
        live_keys = jnp.repeat(entry_live, BLOCK)
        query_tokens = block_id * BLOCK + jnp.arange(BLOCK, dtype=jnp.int32)
        allowed = live_keys[None, :] & (key_tokens[None, :] <= query_tokens[:, None])
        heads_per_query = query_blocks[block_id].astype(jnp.float32)
        head_gradients = grad_blocks[block_id].astype(jnp.float32)
        scores = jnp.einsum("ihd,kd->hik", heads_per_query, key_matrix_rows) * scale
        scores = jnp.where(allowed[None], scores, NEG)
        peak = jnp.max(scores, axis=-1, keepdims=True)
        weights = jnp.exp(scores - peak)
        probs = weights / jnp.sum(weights, axis=-1, keepdims=True)
        reduced_probabilities = probs.astype(jnp.bfloat16)
        attended = jnp.einsum("hik,kd->ihd", reduced_probabilities.astype(jnp.float32), value_matrix_rows).astype(jnp.bfloat16)
        grad_probs = jnp.einsum("ihd,kd->hik", head_gradients, value_matrix_rows)
        delta = jnp.einsum("ihd,ihd->hi", head_gradients, attended.astype(jnp.float32))
        score_gradients = (probs * (grad_probs - delta[:, :, None]) * scale).astype(jnp.bfloat16)
        grad_query = jnp.einsum("hik,kd->ihd", score_gradients.astype(jnp.float32), key_matrix_rows).astype(jnp.bfloat16)
        grad_key = jnp.einsum("hik,ihd->kd", score_gradients.astype(jnp.float32), heads_per_query)
        grad_value = jnp.einsum("hik,ihd->kd", reduced_probabilities.astype(jnp.float32), head_gradients)
        return (attended, grad_query, grad_key.reshape(NB, BLOCK, HEAD_DIM),
                grad_value.reshape(NB, BLOCK, HEAD_DIM), entry_ids)

    attended, grad_queries, grad_key, grad_value, entry_ids = lax.map(one_block, jnp.arange(QBLOCKS, dtype=jnp.int32))
    flat_ids = entry_ids.reshape(-1)
    grad_keys = jax.ops.segment_sum(grad_key.reshape(QBLOCKS * NB, BLOCK, HEAD_DIM), flat_ids, num_segments=QBLOCKS)
    grad_values = jax.ops.segment_sum(grad_value.reshape(QBLOCKS * NB, BLOCK, HEAD_DIM), flat_ids, num_segments=QBLOCKS)
    return (attended.reshape(TOKENS, HEADS * HEAD_DIM), grad_queries.reshape(TOKENS, HEADS * HEAD_DIM),
            grad_keys.reshape(TOKENS, HEAD_DIM), grad_values.reshape(TOKENS, HEAD_DIM))
```

```python
import functools

import jax
import jax.numpy as jnp
from jax import lax
from jax.experimental import pallas as pl
from jax.experimental.pallas import tpu as pltpu
from jax.sharding import PartitionSpec as P

HEADS = 8
HEAD_DIM = 128
BLOCK = 128
STRIPES = 3
BAND = 2
NB = BAND + STRIPES
ROWS = HEADS * BLOCK
PAIR = 2 * BLOCK
NEG = -1e30
SCALE = HEAD_DIM ** (-0.5)
LOG2E = 1.4426950408889634

MESH = pl.DeviceIdType.MESH
BF16 = jnp.bfloat16
F32 = jnp.float32


def nt(x, y):
    return lax.dot_general(x, y, (((1,), (1,)), ((), ())), preferred_element_type=F32)


def nn(x, y):
    return jnp.dot(x, y, preferred_element_type=F32)


def kernel(nb, ni, holders, q_hbm, k_hbm, v_hbm, do_hbm, list_ref,
           att_ref, gq_ref, gk_ref, gv_ref,
           qs, dos, kv, prev, anch, do_t, kall, vall, k_t, v_t, band_s, band_dp, p_s, ds_s, o_t,
           own, mine, gsend, grecv, psend, precv, tsend, trecv, bsend, brecv,
           load_sem, head_sem, band_sem, fwd_send, piece_send, piece_recv, col_send, col_recv,
           back_sem, gcol_send, gcol_recv, gp_send, gp_recv, top_send, top_recv):
    b = lax.axis_index("blk")
    i = lax.axis_index("inner")
    dev = b * ni + i
    piece = PAIR // holders
    last = nb * ni - 1

    def part(n):
        return pl.ds(pl.multiple_of(n * piece, piece), piece)

    barrier = pltpu.get_barrier_semaphore()
    for d in range(1, nb):
        pl.semaphore_signal(barrier, inc=1, device_id=(lax.rem(b + d, nb), i), device_id_type=MESH)
    for d in range(1, ni):
        pl.semaphore_signal(barrier, inc=1, device_id=(b, lax.rem(i + d, ni)), device_id_type=MESH)

    first_of_group = jnp.logical_and(i == 0, b > 0)
    last_of_group = jnp.logical_and(i == ni - 1, b < nb - 1)

    @pl.when(first_of_group)
    def _():
        pl.semaphore_signal(barrier, inc=1, device_id=(b - 1, ni - 1), device_id_type=MESH)

    @pl.when(last_of_group)
    def _():
        pl.semaphore_signal(barrier, inc=1, device_id=(b + 1, 0), device_id_type=MESH)

    load_k = pltpu.make_async_copy(k_hbm, kv.at[pl.ds(0, BLOCK)], load_sem.at[0])
    load_v = pltpu.make_async_copy(v_hbm, kv.at[pl.ds(BLOCK, BLOCK)], load_sem.at[1])
    load_k.start()
    load_v.start()
    head_loads = []
    for h in range(HEADS):
        cols = pl.ds(h * HEAD_DIM, HEAD_DIM)
        rows = pl.ds(h * BLOCK, BLOCK)
        lq = pltpu.make_async_copy(q_hbm.at[:, cols], qs.at[rows], head_sem.at[h])
        ld = pltpu.make_async_copy(do_hbm.at[:, cols], dos.at[rows], head_sem.at[HEADS + h])
        lq.start()
        ld.start()
        head_loads += [lq, ld]
    load_k.wait()
    load_v.wait()

    edges = first_of_group.astype(jnp.int32) + last_of_group.astype(jnp.int32)
    pl.semaphore_wait(barrier, nb - 1 + ni - 1 + edges)

    def piece_copy(source, number, target, sem):
        return pltpu.make_async_remote_copy(
            src_ref=source, dst_ref=anch.at[b, part(number)], send_sem=sem,
            recv_sem=piece_recv.at[number], device_id=(b, target), device_id_type=MESH)

    def scatter_copy(n):
        return piece_copy(kv.at[pl.ds(n * piece, piece)], n, n, fwd_send.at[n])

    def gather_copy(d):
        return piece_copy(anch.at[b, part(i)], i, lax.rem(i + d, ni), piece_send.at[d])

    def root_copy(j):
        return piece_copy(kv.at[pl.ds(0, piece)], 0, j, piece_send.at[j])

    @pl.when(i == 0)
    def _():
        for n in range(1, holders):
            scatter_copy(n).start()
        for j in range(1, ni):
            root_copy(j).start()

    nxt = jnp.minimum(dev + 1, last)
    band = pltpu.make_async_remote_copy(
        src_ref=kv, dst_ref=prev, send_sem=band_sem.at[0], recv_sem=band_sem.at[1],
        device_id=(nxt // ni, lax.rem(nxt, ni)), device_id_type=MESH)

    @pl.when(dev < last)
    def _():
        band.start()

    def column_copy(source, d):
        return pltpu.make_async_remote_copy(
            src_ref=source, dst_ref=anch.at[b], send_sem=col_send.at[d], recv_sem=col_recv.at[b],
            device_id=(b + d, i), device_id_type=MESH)

    def column_wait(a):
        return pltpu.make_async_remote_copy(
            src_ref=kv, dst_ref=anch.at[a], send_sem=col_send.at[0], recv_sem=col_recv.at[a],
            device_id=(lax.rem(b + 1, nb), i), device_id_type=MESH)

    @pl.when(i == 0)
    def _():
        anch[b] = kv[...]
        for d in range(1, nb):
            @pl.when(b + d < nb)
            def _():
                column_copy(kv, d).start()

    @pl.when(dev == 0)
    def _():
        prev[...] = jnp.zeros_like(prev)

    holder = jnp.logical_and(i > 0, i < holders)

    @pl.when(holder)
    def _():
        piece_copy(kv.at[pl.ds(0, piece)], i, lax.rem(i + 1, ni), piece_send.at[0]).wait_recv()
        for d in range(1, ni):
            @pl.when(lax.rem(i + d, ni) != 0)
            def _():
                gather_copy(d).start()

    kall[0:BLOCK] = kv[0:BLOCK]
    vall[0:BLOCK] = kv[BLOCK:PAIR]
    for copy in head_loads:
        copy.wait()
    key_pos = lax.broadcasted_iota(jnp.int32, (BLOCK, PAIR), 0)
    query_pos = lax.rem(lax.broadcasted_iota(jnp.int32, (BLOCK, PAIR), 1), BLOCK)
    causal = key_pos <= query_pos
    for n in range(HEADS // 2):
        sl = slice(n * PAIR, (n + 1) * PAIR)
        band_s[0:BLOCK, sl] = jnp.where(causal, nt(kv[0:BLOCK], qs[sl]), NEG)
        band_dp[0:BLOCK, sl] = nt(kv[BLOCK:PAIR], dos[sl])
    for h in range(HEADS):
        sl = slice(h * BLOCK, (h + 1) * BLOCK)
        do_t[:, sl] = jnp.transpose(dos[sl].astype(F32))

    @pl.when(i > 0)
    def _():
        for d in range(1, holders):
            n = lax.rem(i + d, holders)

            @pl.when(n != i)
            def _():
                piece_copy(kv.at[pl.ds(0, piece)], n, lax.rem(i + 1, ni), piece_send.at[0]).wait_recv()
        for d in range(1, nb):
            @pl.when(b + d < nb)
            def _():
                column_copy(anch.at[b], d).start()

    if holders < ni:
        @pl.when(i >= holders)
        def _():
            n = lax.rem(i, holders)
            piece_copy(kv.at[pl.ds(0, piece)], n, lax.rem(i + 1, ni), piece_send.at[0]).wait_recv()

    @pl.when(dev > 0)
    def _():
        band.wait_recv()

    kall[BLOCK:PAIR] = prev[0:BLOCK]
    vall[BLOCK:PAIR] = prev[BLOCK:PAIR]
    for n in range(HEADS // 2):
        sl = slice(n * PAIR, (n + 1) * PAIR)
        band_s[BLOCK:PAIR, sl] = nt(prev[0:BLOCK], qs[sl])
        band_dp[BLOCK:PAIR, sl] = nt(prev[BLOCK:PAIR], dos[sl])

    for a in range(nb - 1):
        @pl.when(a < b)
        def _():
            column_wait(a).wait_recv()

    listed = [list_ref[0, n] for n in range(NB)]
    prev_live = listed[0] == dev - 1
    for n in range(1, NB):
        prev_live = jnp.logical_or(prev_live, listed[n] == dev - 1)
    prev_live = jnp.logical_and(prev_live, dev > 0)
    biases = [None, jnp.where(prev_live, 0.0, NEG)]
    anchor_ids = []
    for e in range(STRIPES):
        block = listed[BAND + e]
        dead = jnp.logical_or(block == dev, jnp.logical_and(block == dev - 1, prev_live))
        for f in range(e):
            dead = jnp.logical_or(dead, block == listed[BAND + f])
        biases.append(jnp.where(dead, NEG, 0.0))
        anchor_ids.append(block // ni)
        at = slice(PAIR + e * BLOCK, PAIR + (e + 1) * BLOCK)
        picked = anch[anchor_ids[e]]
        kall[at] = picked[0:BLOCK]
        vall[at] = picked[BLOCK:PAIR]
    k_t[...] = jnp.transpose(kall[...].astype(F32)).astype(BF16)
    v_t[...] = jnp.transpose(vall[...].astype(F32)).astype(BF16)

    factor = SCALE * LOG2E
    for n in range(HEADS // 2):
        sl = slice(n * PAIR, (n + 1) * PAIR)
        stripe = nt(kall[PAIR:], qs[sl])
        scores = [band_s[0:BLOCK, sl], band_s[BLOCK:PAIR, sl]]
        scores += [stripe[e * BLOCK:(e + 1) * BLOCK] for e in range(STRIPES)]
        peak = None
        for bias, block in zip(biases, scores):
            top = jnp.max(block, axis=0, keepdims=True)
            if bias is not None:
                top = top + bias
            peak = top if peak is None else jnp.maximum(peak, top)
        peak = peak * factor
        weights = []
        total = None
        for bias, block in zip(biases, scores):
            shift = -peak if bias is None else bias - peak
            weight = jnp.exp2(block * factor + shift)
            weights.append(weight)
            summed = jnp.sum(weight, axis=0, keepdims=True)
            total = summed if total is None else total + summed
        inverse = 1.0 / total
        probs = [weight * inverse for weight in weights]
        for m in range(NB):
            p_s[m * BLOCK:(m + 1) * BLOCK, sl] = probs[m].astype(BF16)
        out = nn(v_t[...], p_s[:, sl]).astype(BF16).astype(F32)
        o_t[:, sl] = out
        delta = jnp.sum(out * do_t[:, sl], axis=0, keepdims=True)
        stripe_dp = nt(vall[PAIR:], dos[sl])
        grads = [band_dp[0:BLOCK, sl], band_dp[BLOCK:PAIR, sl]]
        grads += [stripe_dp[e * BLOCK:(e + 1) * BLOCK] for e in range(STRIPES)]
        for m in range(NB):
            ds_s[m * BLOCK:(m + 1) * BLOCK, sl] = (probs[m] * (grads[m] - delta)).astype(BF16)

    stripe_gk = nn(ds_s[PAIR:, :], qs[...]) * SCALE
    stripe_gv = nn(p_s[PAIR:, :], dos[...])

    def anchor_sum(grad, a):
        total = None
        for e in range(STRIPES):
            term = grad[e * BLOCK:(e + 1) * BLOCK] * jnp.where(anchor_ids[e] == a, 1.0, 0.0)
            total = term if total is None else total + term
        return total

    def gcol_copy(a):
        return pltpu.make_async_remote_copy(
            src_ref=gsend.at[a], dst_ref=grecv.at[b], send_sem=gcol_send.at[a],
            recv_sem=gcol_recv.at[b], device_id=(a, i), device_id_type=MESH)

    def gcol_wait(d):
        return pltpu.make_async_remote_copy(
            src_ref=gsend.at[0], dst_ref=grecv.at[b + d], send_sem=gcol_send.at[0],
            recv_sem=gcol_recv.at[b + d], device_id=(lax.rem(b + 1, nb), i), device_id_type=MESH)

    for a in range(nb - 1):
        @pl.when(a < b)
        def _():
            gsend[a, 0:BLOCK] = anchor_sum(stripe_gk, a).astype(BF16)
            gsend[a, BLOCK:PAIR] = anchor_sum(stripe_gv, a).astype(BF16)
            gcol_copy(a).start()
    mine[0:BLOCK] = anchor_sum(stripe_gk, b)
    mine[BLOCK:PAIR] = anchor_sum(stripe_gv, b)

    band_gk = nn(ds_s[0:PAIR, :], qs[...]) * SCALE
    band_gv = nn(p_s[0:PAIR, :], dos[...])
    own[0:BLOCK] = band_gk[0:BLOCK]
    own[BLOCK:PAIR] = band_gv[0:BLOCK]
    bsend[0:BLOCK] = band_gk[BLOCK:PAIR].astype(BF16)
    bsend[BLOCK:PAIR] = band_gv[BLOCK:PAIR].astype(BF16)
    before = jnp.maximum(dev - 1, 0)
    back = pltpu.make_async_remote_copy(
        src_ref=bsend, dst_ref=brecv, send_sem=back_sem.at[0], recv_sem=back_sem.at[1],
        device_id=(before // ni, lax.rem(before, ni)), device_id_type=MESH)

    @pl.when(dev > 0)
    def _():
        back.start()

    for d in range(1, nb):
        @pl.when(b + d < nb)
        def _():
            gcol_wait(d).wait_recv()
            mine[...] += grecv[b + d].astype(F32)
    psend[...] = mine[...].astype(BF16)

    def gp_copy(d):
        n = lax.rem(i + d, ni)
        return pltpu.make_async_remote_copy(
            src_ref=psend.at[part(n)], dst_ref=precv.at[i], send_sem=gp_send.at[d],
            recv_sem=gp_recv.at[i], device_id=(b, n), device_id_type=MESH)

    def gp_wait(d):
        n = lax.rem(i + d, ni)
        return pltpu.make_async_remote_copy(
            src_ref=psend.at[pl.ds(0, piece)], dst_ref=precv.at[n], send_sem=gp_send.at[0],
            recv_sem=gp_recv.at[n], device_id=(b, n), device_id_type=MESH)

    for d in range(1, ni):
        @pl.when(lax.rem(i + d, ni) < holders)
        def _():
            gp_copy(d).start()

    def write_heads(heads):
        for h in heads:
            sl = slice(h * BLOCK, (h + 1) * BLOCK)
            gq = nn(k_t[...], ds_s[:, sl]) * SCALE
            gq_ref[:, sl] = jnp.transpose(gq).astype(BF16)
            att_ref[:, sl] = jnp.transpose(o_t[:, sl]).astype(BF16)

    write_heads(range(0, HEADS // 2))

    def top_copy(n):
        return pltpu.make_async_remote_copy(
            src_ref=tsend, dst_ref=trecv.at[n], send_sem=top_send.at[0], recv_sem=top_recv.at[n],
            device_id=(b, 0), device_id_type=MESH)

    def top_wait(n):
        return pltpu.make_async_remote_copy(
            src_ref=tsend, dst_ref=trecv.at[n], send_sem=top_send.at[0], recv_sem=top_recv.at[n],
            device_id=(b, n), device_id_type=MESH)

    @pl.when(i < holders)
    def _():
        total = mine[part(i)]
        for d in range(1, ni):
            gp_wait(d).wait_recv()
            total = total + precv[lax.rem(i + d, ni)].astype(F32)
        tsend[...] = total

        @pl.when(i > 0)
        def _():
            top_copy(i).start()

    write_heads(range(HEADS // 2, HEADS))

    @pl.when(dev < last)
    def _():
        back.wait_recv()
        own[...] += brecv[...].astype(F32)

    @pl.when(i == 0)
    def _():
        own[0:piece] += tsend[...]
        for n in range(1, holders):
            top_wait(n).wait_recv()
            own[n * piece:(n + 1) * piece] += trecv[n]

    gk_ref[...] = own[0:BLOCK]
    gv_ref[...] = own[BLOCK:PAIR]

    @pl.when(dev < last)
    def _():
        band.wait_send()

    @pl.when(dev > 0)
    def _():
        back.wait_send()

    @pl.when(i == 0)
    def _():
        for n in range(1, holders):
            scatter_copy(n).wait_send()
        for j in range(1, ni):
            root_copy(j).wait_send()

    @pl.when(holder)
    def _():
        for d in range(1, ni):
            @pl.when(lax.rem(i + d, ni) != 0)
            def _():
                gather_copy(d).wait_send()
        top_copy(i).wait_send()

    for d in range(1, nb):
        @pl.when(b + d < nb)
        def _():
            column_copy(kv, d).wait_send()
    for a in range(nb - 1):
        @pl.when(a < b)
        def _():
            gcol_copy(a).wait_send()
    for d in range(1, ni):
        @pl.when(lax.rem(i + d, ni) < holders)
        def _():
            gp_copy(d).wait_send()


def solution(mesh):
    nb, ni = mesh.shape["blk"], mesh.shape["inner"]
    holders = min(ni, 8)
    piece = PAIR // holders
    dma = pltpu.SemaphoreType.DMA

    def shards(queries, keys, values, out_grad, block_list):
        any_spec = pl.BlockSpec(memory_space=pl.ANY)
        vmem_spec = pl.BlockSpec(memory_space=pltpu.VMEM)
        return pl.pallas_call(
            functools.partial(kernel, nb, ni, holders),
            out_shape=(
                jax.ShapeDtypeStruct((BLOCK, ROWS), BF16),
                jax.ShapeDtypeStruct((BLOCK, ROWS), BF16),
                jax.ShapeDtypeStruct((BLOCK, HEAD_DIM), F32),
                jax.ShapeDtypeStruct((BLOCK, HEAD_DIM), F32),
            ),
            in_specs=[any_spec] * 4 + [pl.BlockSpec(memory_space=pltpu.SMEM)],
            out_specs=(vmem_spec,) * 4,
            scratch_shapes=[
                pltpu.VMEM((ROWS, HEAD_DIM), BF16),
                pltpu.VMEM((ROWS, HEAD_DIM), BF16),
                pltpu.VMEM((PAIR, HEAD_DIM), BF16),
                pltpu.VMEM((PAIR, HEAD_DIM), BF16),
                pltpu.VMEM((nb, PAIR, HEAD_DIM), BF16),
                pltpu.VMEM((HEAD_DIM, ROWS), F32),
                pltpu.VMEM((NB * BLOCK, HEAD_DIM), BF16),
                pltpu.VMEM((NB * BLOCK, HEAD_DIM), BF16),
                pltpu.VMEM((HEAD_DIM, NB * BLOCK), BF16),
                pltpu.VMEM((HEAD_DIM, NB * BLOCK), BF16),
                pltpu.VMEM((PAIR, ROWS), F32),
                pltpu.VMEM((PAIR, ROWS), F32),
                pltpu.VMEM((NB * BLOCK, ROWS), BF16),
                pltpu.VMEM((NB * BLOCK, ROWS), BF16),
                pltpu.VMEM((HEAD_DIM, ROWS), F32),
                pltpu.VMEM((PAIR, HEAD_DIM), F32),
                pltpu.VMEM((PAIR, HEAD_DIM), F32),
                pltpu.VMEM((nb, PAIR, HEAD_DIM), BF16),
                pltpu.VMEM((nb, PAIR, HEAD_DIM), BF16),
                pltpu.VMEM((PAIR, HEAD_DIM), BF16),
                pltpu.VMEM((ni, piece, HEAD_DIM), BF16),
                pltpu.VMEM((piece, HEAD_DIM), F32),
                pltpu.VMEM((holders, piece, HEAD_DIM), F32),
                pltpu.VMEM((PAIR, HEAD_DIM), BF16),
                pltpu.VMEM((PAIR, HEAD_DIM), BF16),
                dma((2,)),
                dma((2 * HEADS,)),
                dma((2,)),
                dma((holders,)),
                dma((ni,)),
                dma((holders,)),
                dma((nb,)),
                dma((nb,)),
                dma((2,)),
                dma((nb,)),
                dma((nb,)),
                dma((ni,)),
                dma((ni,)),
                dma((1,)),
                dma((holders,)),
            ],
            compiler_params=pltpu.CompilerParams(
                collective_id=0, has_side_effects=True, vmem_limit_bytes=40 * 1024 * 1024
            ),
            name="sparse_attention",
        )(queries, keys, values, out_grad, block_list)

    spec = P(("blk", "inner"), None)
    return jax.shard_map(
        shards, mesh=mesh, in_specs=(spec,) * 5, out_specs=(spec,) * 4, check_vma=False
    )
```

```python
import functools

import jax
import jax.numpy as jnp
from jax import lax
from jax.experimental import pallas as pl
from jax.experimental.pallas import tpu as pltpu
from jax.sharding import PartitionSpec as P

HEADS = 8
HEAD_DIM = 128
BLOCK = 128
STRIPES = 3
BAND = 2
NB = BAND + STRIPES
ROWS = HEADS * BLOCK
PAIR = 2 * BLOCK
NEG = -1e30
SCALE = HEAD_DIM ** (-0.5)
LOG2E = 1.4426950408889634

MESH = pl.DeviceIdType.MESH
BF16 = jnp.bfloat16
F32 = jnp.float32


def nt(x, y):
    return lax.dot_general(x, y, (((1,), (1,)), ((), ())), preferred_element_type=F32)


def nn(x, y):
    return jnp.dot(x, y, preferred_element_type=F32)


def kernel(nb, ni, holders, q_hbm, k_hbm, v_hbm, do_hbm, list_ref,
           att_ref, gq_ref, gk_ref, gv_ref,
           qs, dos, kv, prev, anch, do_t, kall, vall, k_t, v_t, band_s, band_dp, p_s, ds_s, o_t,
           own, mine, gsend, grecv, psend, precv, total_ref, tsend, trecv, bsend, brecv,
           load_sem, head_sem, band_sem, fwd_send, piece_send, piece_recv, col_send, col_recv,
           back_sem, gcol_send, gcol_recv, gp_send, gp_recv, top_send, top_recv):
    b = lax.axis_index("blk")
    i = lax.axis_index("inner")
    dev = b * ni + i
    piece = PAIR // holders
    last = nb * ni - 1

    def part(n):
        return pl.ds(pl.multiple_of(n * piece, piece), piece)

    barrier = pltpu.get_barrier_semaphore()
    for d in range(1, nb):
        pl.semaphore_signal(barrier, inc=1, device_id=(lax.rem(b + d, nb), i), device_id_type=MESH)
    for d in range(1, ni):
        pl.semaphore_signal(barrier, inc=1, device_id=(b, lax.rem(i + d, ni)), device_id_type=MESH)

    first_of_group = jnp.logical_and(i == 0, b > 0)
    last_of_group = jnp.logical_and(i == ni - 1, b < nb - 1)

    @pl.when(first_of_group)
    def _():
        pl.semaphore_signal(barrier, inc=1, device_id=(b - 1, ni - 1), device_id_type=MESH)

    @pl.when(last_of_group)
    def _():
        pl.semaphore_signal(barrier, inc=1, device_id=(b + 1, 0), device_id_type=MESH)

    load_k = pltpu.make_async_copy(k_hbm, kv.at[pl.ds(0, BLOCK)], load_sem.at[0])
    load_v = pltpu.make_async_copy(v_hbm, kv.at[pl.ds(BLOCK, BLOCK)], load_sem.at[1])
    load_k.start()
    load_v.start()
    head_loads = []
    for h in range(HEADS):
        cols = pl.ds(h * HEAD_DIM, HEAD_DIM)
        rows = pl.ds(h * BLOCK, BLOCK)
        lq = pltpu.make_async_copy(q_hbm.at[:, cols], qs.at[rows], head_sem.at[h])
        ld = pltpu.make_async_copy(do_hbm.at[:, cols], dos.at[rows], head_sem.at[HEADS + h])
        lq.start()
        ld.start()
        head_loads += [lq, ld]
    load_k.wait()
    load_v.wait()

    edges = first_of_group.astype(jnp.int32) + last_of_group.astype(jnp.int32)
    pl.semaphore_wait(barrier, nb - 1 + ni - 1 + edges)

    def piece_copy(source, number, target, sem):
        return pltpu.make_async_remote_copy(
            src_ref=source, dst_ref=anch.at[b, part(number)], send_sem=sem,
            recv_sem=piece_recv.at[number], device_id=(b, target), device_id_type=MESH)

    def scatter_copy(n):
        return piece_copy(kv.at[pl.ds(n * piece, piece)], n, n, fwd_send.at[n])

    def gather_copy(d):
        return piece_copy(anch.at[b, part(i)], i, lax.rem(i + d, ni), piece_send.at[d])

    def root_copy(j):
        return piece_copy(kv.at[pl.ds(0, piece)], 0, j, piece_send.at[j])

    @pl.when(i == 0)
    def _():
        for n in range(1, holders):
            scatter_copy(n).start()
        for j in range(1, ni):
            root_copy(j).start()

    nxt = jnp.minimum(dev + 1, last)
    band = pltpu.make_async_remote_copy(
        src_ref=kv, dst_ref=prev, send_sem=band_sem.at[0], recv_sem=band_sem.at[1],
        device_id=(nxt // ni, lax.rem(nxt, ni)), device_id_type=MESH)

    def root_column(d):
        return pltpu.make_async_remote_copy(
            src_ref=kv, dst_ref=anch.at[b], send_sem=col_send.at[d, 0], recv_sem=col_recv.at[b, 0],
            device_id=(b + d, i), device_id_type=MESH)

    def column_copy(n, d):
        return pltpu.make_async_remote_copy(
            src_ref=anch.at[b, part(n)], dst_ref=anch.at[b, part(n)], send_sem=col_send.at[d, n],
            recv_sem=col_recv.at[b, n], device_id=(b + d, i), device_id_type=MESH)

    def root_column_wait(a):
        return pltpu.make_async_remote_copy(
            src_ref=kv, dst_ref=anch.at[a], send_sem=col_send.at[0, 0], recv_sem=col_recv.at[a, 0],
            device_id=(lax.rem(b + 1, nb), i), device_id_type=MESH)

    def column_wait(a, n):
        return pltpu.make_async_remote_copy(
            src_ref=kv.at[pl.ds(0, piece)], dst_ref=anch.at[a, pl.ds(n * piece, piece)],
            send_sem=col_send.at[0, 0], recv_sem=col_recv.at[a, n],
            device_id=(lax.rem(b + 1, nb), i), device_id_type=MESH)

    @pl.when(i == 0)
    def _():
        anch[b] = kv[...]
        for d in range(1, nb):
            @pl.when(b + d < nb)
            def _():
                root_column(d).start()

    @pl.when(dev == 0)
    def _():
        prev[...] = jnp.zeros_like(prev)

    holder = jnp.logical_and(i > 0, i < holders)

    @pl.when(holder)
    def _():
        piece_copy(kv.at[pl.ds(0, piece)], i, lax.rem(i + 1, ni), piece_send.at[0]).wait_recv()
        for d in range(1, ni):
            @pl.when(lax.rem(i + d, ni) != 0)
            def _():
                gather_copy(d).start()
        for d in range(1, nb):
            @pl.when(b + d < nb)
            def _():
                column_copy(i, d).start()

    @pl.when(dev < last)
    def _():
        band.start()

    kall[0:BLOCK] = kv[0:BLOCK]
    vall[0:BLOCK] = kv[BLOCK:PAIR]
    for copy in head_loads:
        copy.wait()
    key_pos = lax.broadcasted_iota(jnp.int32, (BLOCK, PAIR), 0)
    query_pos = lax.rem(lax.broadcasted_iota(jnp.int32, (BLOCK, PAIR), 1), BLOCK)
    causal = key_pos <= query_pos
    for n in range(HEADS // 2):
        sl = slice(n * PAIR, (n + 1) * PAIR)
        band_s[0:BLOCK, sl] = jnp.where(causal, nt(kv[0:BLOCK], qs[sl]), NEG)
        band_dp[0:BLOCK, sl] = nt(kv[BLOCK:PAIR], dos[sl])
    for h in range(HEADS):
        sl = slice(h * BLOCK, (h + 1) * BLOCK)
        do_t[:, sl] = jnp.transpose(dos[sl].astype(F32))

    @pl.when(i > 0)
    def _():
        for t in range(1, holders):
            n = lax.rem(i + t, holders)

            @pl.when(n != i)
            def _():
                piece_copy(kv.at[pl.ds(0, piece)], n, lax.rem(i + 1, ni), piece_send.at[0]).wait_recv()
            for d in range(1, nb):
                @pl.when(b + d < nb)
                def _():
                    column_copy(n, d).start()

    if holders < ni:
        @pl.when(i >= holders)
        def _():
            n = lax.rem(i, holders)
            piece_copy(kv.at[pl.ds(0, piece)], n, lax.rem(i + 1, ni), piece_send.at[0]).wait_recv()
            for d in range(1, nb):
                @pl.when(b + d < nb)
                def _():
                    column_copy(n, d).start()

    @pl.when(dev > 0)
    def _():
        band.wait_recv()

    kall[BLOCK:PAIR] = prev[0:BLOCK]
    vall[BLOCK:PAIR] = prev[BLOCK:PAIR]
    for n in range(HEADS // 2):
        sl = slice(n * PAIR, (n + 1) * PAIR)
        band_s[BLOCK:PAIR, sl] = nt(prev[0:BLOCK], qs[sl])
        band_dp[BLOCK:PAIR, sl] = nt(prev[BLOCK:PAIR], dos[sl])

    for a in range(nb - 1):
        @pl.when(a < b)
        def _():
            @pl.when(i == 0)
            def _():
                root_column_wait(a).wait_recv()

            @pl.when(i > 0)
            def _():
                for n in range(holders):
                    column_wait(a, n).wait_recv()

    listed = [list_ref[0, n] for n in range(NB)]
    prev_live = listed[0] == dev - 1
    for n in range(1, NB):
        prev_live = jnp.logical_or(prev_live, listed[n] == dev - 1)
    prev_live = jnp.logical_and(prev_live, dev > 0)
    biases = [None, jnp.where(prev_live, 0.0, NEG)]
    anchor_ids = []
    for e in range(STRIPES):
        block = listed[BAND + e]
        dead = jnp.logical_or(block == dev, jnp.logical_and(block == dev - 1, prev_live))
        for f in range(e):
            dead = jnp.logical_or(dead, block == listed[BAND + f])
        biases.append(jnp.where(dead, NEG, 0.0))
        anchor_ids.append(block // ni)
        at = slice(PAIR + e * BLOCK, PAIR + (e + 1) * BLOCK)
        picked = anch[anchor_ids[e]]
        kall[at] = picked[0:BLOCK]
        vall[at] = picked[BLOCK:PAIR]
    k_t[...] = jnp.transpose(kall[...].astype(F32)).astype(BF16)
    v_t[...] = jnp.transpose(vall[...].astype(F32)).astype(BF16)

    factor = SCALE * LOG2E
    for n in range(HEADS // 2):
        sl = slice(n * PAIR, (n + 1) * PAIR)
        stripe = nt(kall[PAIR:], qs[sl])
        scores = [band_s[0:BLOCK, sl], band_s[BLOCK:PAIR, sl]]
        scores += [stripe[e * BLOCK:(e + 1) * BLOCK] for e in range(STRIPES)]
        peak = None
        for bias, block in zip(biases, scores):
            top = jnp.max(block, axis=0, keepdims=True)
            if bias is not None:
                top = top + bias
            peak = top if peak is None else jnp.maximum(peak, top)
        peak = peak * factor
        weights = []
        total = None
        for bias, block in zip(biases, scores):
            shift = -peak if bias is None else bias - peak
            weight = jnp.exp2(block * factor + shift)
            weights.append(weight)
            summed = jnp.sum(weight, axis=0, keepdims=True)
            total = summed if total is None else total + summed
        inverse = 1.0 / total
        probs = [weight * inverse for weight in weights]
        for m in range(NB):
            p_s[m * BLOCK:(m + 1) * BLOCK, sl] = probs[m].astype(BF16)
        out = nn(v_t[...], p_s[:, sl]).astype(BF16).astype(F32)
        o_t[:, sl] = out
        delta = jnp.sum(out * do_t[:, sl], axis=0, keepdims=True)
        stripe_dp = nt(vall[PAIR:], dos[sl])
        grads = [band_dp[0:BLOCK, sl], band_dp[BLOCK:PAIR, sl]]
        grads += [stripe_dp[e * BLOCK:(e + 1) * BLOCK] for e in range(STRIPES)]
        for m in range(NB):
            ds_s[m * BLOCK:(m + 1) * BLOCK, sl] = (probs[m] * (grads[m] - delta)).astype(BF16)

    stripe_gk = nn(ds_s[PAIR:, :], qs[...]) * SCALE
    stripe_gv = nn(p_s[PAIR:, :], dos[...])

    def anchor_sum(grad, a):
        total = None
        for e in range(STRIPES):
            term = grad[e * BLOCK:(e + 1) * BLOCK] * jnp.where(anchor_ids[e] == a, 1.0, 0.0)
            total = term if total is None else total + term
        return total

    def gcol_copy(a):
        return pltpu.make_async_remote_copy(
            src_ref=gsend.at[a], dst_ref=grecv.at[b], send_sem=gcol_send.at[a],
            recv_sem=gcol_recv.at[b], device_id=(a, i), device_id_type=MESH)

    def gcol_wait(d):
        return pltpu.make_async_remote_copy(
            src_ref=gsend.at[0], dst_ref=grecv.at[b + d], send_sem=gcol_send.at[0],
            recv_sem=gcol_recv.at[b + d], device_id=(lax.rem(b + 1, nb), i), device_id_type=MESH)

    for a in range(nb - 1):
        @pl.when(a < b)
        def _():
            gsend[a, 0:BLOCK] = anchor_sum(stripe_gk, a).astype(BF16)
            gsend[a, BLOCK:PAIR] = anchor_sum(stripe_gv, a).astype(BF16)
            gcol_copy(a).start()
    mine[0:BLOCK] = anchor_sum(stripe_gk, b)
    mine[BLOCK:PAIR] = anchor_sum(stripe_gv, b)

    band_gk = nn(ds_s[0:PAIR, :], qs[...]) * SCALE
    band_gv = nn(p_s[0:PAIR, :], dos[...])
    own[0:BLOCK] = band_gk[0:BLOCK]
    own[BLOCK:PAIR] = band_gv[0:BLOCK]
    bsend[0:BLOCK] = band_gk[BLOCK:PAIR].astype(BF16)
    bsend[BLOCK:PAIR] = band_gv[BLOCK:PAIR].astype(BF16)
    before = jnp.maximum(dev - 1, 0)
    back = pltpu.make_async_remote_copy(
        src_ref=bsend, dst_ref=brecv, send_sem=back_sem.at[0], recv_sem=back_sem.at[1],
        device_id=(before // ni, lax.rem(before, ni)), device_id_type=MESH)

    for d in range(1, nb):
        @pl.when(b + d < nb)
        def _():
            gcol_wait(d).wait_recv()
            mine[...] += grecv[b + d].astype(F32)
    psend[...] = mine[...].astype(BF16)

    def gp_copy(d):
        n = lax.rem(i + d, ni)
        return pltpu.make_async_remote_copy(
            src_ref=psend.at[part(n)], dst_ref=precv.at[i], send_sem=gp_send.at[d],
            recv_sem=gp_recv.at[i], device_id=(b, n), device_id_type=MESH)

    def gp_wait(d):
        n = lax.rem(i + d, ni)
        return pltpu.make_async_remote_copy(
            src_ref=psend.at[pl.ds(0, piece)], dst_ref=precv.at[n], send_sem=gp_send.at[0],
            recv_sem=gp_recv.at[n], device_id=(b, n), device_id_type=MESH)

    for d in range(1, ni):
        @pl.when(lax.rem(i + d, ni) < holders)
        def _():
            gp_copy(d).start()

    @pl.when(dev > 0)
    def _():
        back.start()

    def write_heads(heads):
        for h in heads:
            sl = slice(h * BLOCK, (h + 1) * BLOCK)
            gq = nn(k_t[...], ds_s[:, sl]) * SCALE
            gq_ref[:, sl] = jnp.transpose(gq).astype(BF16)
            att_ref[:, sl] = jnp.transpose(o_t[:, sl]).astype(BF16)

    write_heads(range(0, HEADS // 2))

    def top_copy(n):
        return pltpu.make_async_remote_copy(
            src_ref=tsend, dst_ref=trecv.at[n], send_sem=top_send.at[0], recv_sem=top_recv.at[n],
            device_id=(b, 0), device_id_type=MESH)

    def top_wait(n):
        return pltpu.make_async_remote_copy(
            src_ref=tsend, dst_ref=trecv.at[n], send_sem=top_send.at[0], recv_sem=top_recv.at[n],
            device_id=(b, n), device_id_type=MESH)

    @pl.when(i < holders)
    def _():
        total = mine[part(i)]
        for d in range(1, ni):
            gp_wait(d).wait_recv()
            total = total + precv[lax.rem(i + d, ni)].astype(F32)
        total_ref[...] = total
        tsend[...] = total.astype(BF16)

        @pl.when(i > 0)
        def _():
            top_copy(i).start()

    write_heads(range(HEADS // 2, HEADS))

    @pl.when(dev < last)
    def _():
        back.wait_recv()
        own[...] += brecv[...].astype(F32)

    @pl.when(i == 0)
    def _():
        own[0:piece] += total_ref[...]
        for n in range(1, holders):
            top_wait(n).wait_recv()
            own[n * piece:(n + 1) * piece] += trecv[n].astype(F32)

    gk_ref[...] = own[0:BLOCK]
    gv_ref[...] = own[BLOCK:PAIR]

    @pl.when(dev < last)
    def _():
        band.wait_send()

    @pl.when(dev > 0)
    def _():
        back.wait_send()

    @pl.when(i == 0)
    def _():
        for n in range(1, holders):
            scatter_copy(n).wait_send()
        for j in range(1, ni):
            root_copy(j).wait_send()

    @pl.when(holder)
    def _():
        for d in range(1, ni):
            @pl.when(lax.rem(i + d, ni) != 0)
            def _():
                gather_copy(d).wait_send()
        top_copy(i).wait_send()

    for d in range(1, nb):
        @pl.when(b + d < nb)
        def _():
            @pl.when(i == 0)
            def _():
                root_column(d).wait_send()

            @pl.when(i > 0)
            def _():
                for n in range(holders):
                    column_copy(n, d).wait_send()
    for a in range(nb - 1):
        @pl.when(a < b)
        def _():
            gcol_copy(a).wait_send()
    for d in range(1, ni):
        @pl.when(lax.rem(i + d, ni) < holders)
        def _():
            gp_copy(d).wait_send()


def write_out(*refs):
    for n in range(4):
        refs[4 + n][...] = refs[n][...]


def solution(mesh):
    nb, ni = mesh.shape["blk"], mesh.shape["inner"]
    holders = min(ni, 8)
    piece = PAIR // holders
    dma = pltpu.SemaphoreType.DMA

    def shards(queries, keys, values, out_grad, block_list):
        any_spec = pl.BlockSpec(memory_space=pl.ANY)
        vmem_spec = pl.BlockSpec(memory_space=pltpu.VMEM)
        results = pl.pallas_call(
            functools.partial(kernel, nb, ni, holders),
            out_shape=(
                jax.ShapeDtypeStruct((BLOCK, ROWS), BF16),
                jax.ShapeDtypeStruct((BLOCK, ROWS), BF16),
                jax.ShapeDtypeStruct((BLOCK, HEAD_DIM), F32),
                jax.ShapeDtypeStruct((BLOCK, HEAD_DIM), F32),
            ),
            in_specs=[any_spec] * 4 + [pl.BlockSpec(memory_space=pltpu.SMEM)],
            out_specs=(vmem_spec,) * 4,
            scratch_shapes=[
                pltpu.VMEM((ROWS, HEAD_DIM), BF16),
                pltpu.VMEM((ROWS, HEAD_DIM), BF16),
                pltpu.VMEM((PAIR, HEAD_DIM), BF16),
                pltpu.VMEM((PAIR, HEAD_DIM), BF16),
                pltpu.VMEM((nb, PAIR, HEAD_DIM), BF16),
                pltpu.VMEM((HEAD_DIM, ROWS), F32),
                pltpu.VMEM((NB * BLOCK, HEAD_DIM), BF16),
                pltpu.VMEM((NB * BLOCK, HEAD_DIM), BF16),
                pltpu.VMEM((HEAD_DIM, NB * BLOCK), BF16),
                pltpu.VMEM((HEAD_DIM, NB * BLOCK), BF16),
                pltpu.VMEM((PAIR, ROWS), F32),
                pltpu.VMEM((PAIR, ROWS), F32),
                pltpu.VMEM((NB * BLOCK, ROWS), BF16),
                pltpu.VMEM((NB * BLOCK, ROWS), BF16),
                pltpu.VMEM((HEAD_DIM, ROWS), F32),
                pltpu.VMEM((PAIR, HEAD_DIM), F32),
                pltpu.VMEM((PAIR, HEAD_DIM), F32),
                pltpu.VMEM((nb, PAIR, HEAD_DIM), BF16),
                pltpu.VMEM((nb, PAIR, HEAD_DIM), BF16),
                pltpu.VMEM((PAIR, HEAD_DIM), BF16),
                pltpu.VMEM((ni, piece, HEAD_DIM), BF16),
                pltpu.VMEM((piece, HEAD_DIM), F32),
                pltpu.VMEM((piece, HEAD_DIM), BF16),
                pltpu.VMEM((holders, piece, HEAD_DIM), BF16),
                pltpu.VMEM((PAIR, HEAD_DIM), BF16),
                pltpu.VMEM((PAIR, HEAD_DIM), BF16),
                dma((2,)),
                dma((2 * HEADS,)),
                dma((2,)),
                dma((holders,)),
                dma((ni,)),
                dma((holders,)),
                dma((nb, holders)),
                dma((nb, holders)),
                dma((2,)),
                dma((nb,)),
                dma((nb,)),
                dma((ni,)),
                dma((ni,)),
                dma((1,)),
                dma((holders,)),
            ],
            compiler_params=pltpu.CompilerParams(
                collective_id=0, has_side_effects=True, vmem_limit_bytes=60 * 1024 * 1024
            ),
            name="sparse_attention",
        )(queries, keys, values, out_grad, block_list)
        return pl.pallas_call(
            write_out,
            out_shape=tuple(jax.ShapeDtypeStruct(r.shape, r.dtype) for r in results),
            in_specs=[vmem_spec] * 4,
            out_specs=(vmem_spec,) * 4,
            name="write_out",
        )(*results)

    spec = P(("blk", "inner"), None)
    return jax.shard_map(
        shards, mesh=mesh, in_specs=(spec,) * 5, out_specs=(spec,) * 4, check_vma=False
    )
```

```python
import functools

import jax
import jax.numpy as jnp
from jax import lax
from jax.experimental import pallas as pl
from jax.experimental.pallas import tpu as pltpu
from jax.sharding import PartitionSpec as P

HEADS = 8
HEAD_DIM = 128
BLOCK = 128
STRIPES = 3
BAND = 2
NB = BAND + STRIPES
ROWS = HEADS * BLOCK
PAIR = 2 * BLOCK
NEG = -1e30
SCALE = HEAD_DIM ** (-0.5)
LOG2E = 1.4426950408889634

MESH = pl.DeviceIdType.MESH
BF16 = jnp.bfloat16
F32 = jnp.float32


def nt(x, y):
    return lax.dot_general(x, y, (((1,), (1,)), ((), ())), preferred_element_type=F32)


def nn(x, y):
    return jnp.dot(x, y, preferred_element_type=F32)


def kernel(nb, ni, holders, q_hbm, k_hbm, v_hbm, do_hbm, list_ref,
           att_ref, gq_ref, gk_ref, gv_ref,
           qs, dos, kv, prev, anch, do_t, kall, vall, k_t, v_t, band_s, band_dp, stat, p_s, ds_s, o_t,
           own, mine, gsend, grecv, psend, precv, total_ref, tsend, trecv, bsend, brecv,
           load_sem, head_sem, band_sem, fwd_send, piece_send, piece_recv, col_send, col_recv,
           back_sem, gcol_send, gcol_recv, gp_send, gp_recv, top_send, top_recv):
    b = lax.axis_index("blk")
    i = lax.axis_index("inner")
    dev = b * ni + i
    piece = PAIR // holders
    last = nb * ni - 1

    def part(n):
        return pl.ds(pl.multiple_of(n * piece, piece), piece)

    barrier = pltpu.get_barrier_semaphore()
    for d in range(1, nb):
        pl.semaphore_signal(barrier, inc=1, device_id=(lax.rem(b + d, nb), i), device_id_type=MESH)
    for d in range(1, ni):
        pl.semaphore_signal(barrier, inc=1, device_id=(b, lax.rem(i + d, ni)), device_id_type=MESH)

    first_of_group = jnp.logical_and(i == 0, b > 0)
    last_of_group = jnp.logical_and(i == ni - 1, b < nb - 1)

    @pl.when(first_of_group)
    def _():
        pl.semaphore_signal(barrier, inc=1, device_id=(b - 1, ni - 1), device_id_type=MESH)

    @pl.when(last_of_group)
    def _():
        pl.semaphore_signal(barrier, inc=1, device_id=(b + 1, 0), device_id_type=MESH)

    load_k = pltpu.make_async_copy(k_hbm, kv.at[pl.ds(0, BLOCK)], load_sem.at[0])
    load_v = pltpu.make_async_copy(v_hbm, kv.at[pl.ds(BLOCK, BLOCK)], load_sem.at[1])
    load_k.start()
    load_v.start()
    head_loads = []
    for h in range(HEADS):
        cols = pl.ds(h * HEAD_DIM, HEAD_DIM)
        rows = pl.ds(h * BLOCK, BLOCK)
        lq = pltpu.make_async_copy(q_hbm.at[:, cols], qs.at[rows], head_sem.at[h])
        ld = pltpu.make_async_copy(do_hbm.at[:, cols], dos.at[rows], head_sem.at[HEADS + h])
        lq.start()
        ld.start()
        head_loads += [lq, ld]
    load_k.wait()
    load_v.wait()

    edges = first_of_group.astype(jnp.int32) + last_of_group.astype(jnp.int32)
    pl.semaphore_wait(barrier, nb - 1 + ni - 1 + edges)

    def piece_copy(source, number, target, sem):
        return pltpu.make_async_remote_copy(
            src_ref=source, dst_ref=anch.at[b, part(number)], send_sem=sem,
            recv_sem=piece_recv.at[number], device_id=(b, target), device_id_type=MESH)

    def scatter_copy(n):
        return piece_copy(kv.at[pl.ds(n * piece, piece)], n, n, fwd_send.at[n])

    def gather_copy(d):
        return piece_copy(anch.at[b, part(i)], i, lax.rem(i + d, ni), piece_send.at[d])

    def root_copy(j):
        return piece_copy(kv.at[pl.ds(0, piece)], 0, j, piece_send.at[j])

    @pl.when(i == 0)
    def _():
        for n in range(1, holders):
            scatter_copy(n).start()
        for j in range(1, ni):
            root_copy(j).start()

    nxt = jnp.minimum(dev + 1, last)
    band = pltpu.make_async_remote_copy(
        src_ref=kv, dst_ref=prev, send_sem=band_sem.at[0], recv_sem=band_sem.at[1],
        device_id=(nxt // ni, lax.rem(nxt, ni)), device_id_type=MESH)

    @pl.when(jnp.logical_and(dev < last, i > 0))
    def _():
        band.start()

    def root_column(d):
        return pltpu.make_async_remote_copy(
            src_ref=kv, dst_ref=anch.at[b], send_sem=col_send.at[d, 0], recv_sem=col_recv.at[b, 0],
            device_id=(b + d, i), device_id_type=MESH)

    def column_copy(n, d):
        return pltpu.make_async_remote_copy(
            src_ref=anch.at[b, part(n)], dst_ref=anch.at[b, part(n)], send_sem=col_send.at[d, n],
            recv_sem=col_recv.at[b, n], device_id=(b + d, i), device_id_type=MESH)

    def root_column_wait(a):
        return pltpu.make_async_remote_copy(
            src_ref=kv, dst_ref=anch.at[a], send_sem=col_send.at[0, 0], recv_sem=col_recv.at[a, 0],
            device_id=(lax.rem(b + 1, nb), i), device_id_type=MESH)

    def column_wait(a, n):
        return pltpu.make_async_remote_copy(
            src_ref=kv.at[pl.ds(0, piece)], dst_ref=anch.at[a, pl.ds(n * piece, piece)],
            send_sem=col_send.at[0, 0], recv_sem=col_recv.at[a, n],
            device_id=(lax.rem(b + 1, nb), i), device_id_type=MESH)

    @pl.when(i == 0)
    def _():
        anch[b] = kv[...]
        for d in range(1, nb):
            @pl.when(b + d < nb)
            def _():
                root_column(d).start()

        @pl.when(dev < last)
        def _():
            band.start()

    @pl.when(dev == 0)
    def _():
        prev[...] = jnp.zeros_like(prev)

    holder = jnp.logical_and(i > 0, i < holders)

    @pl.when(holder)
    def _():
        piece_copy(kv.at[pl.ds(0, piece)], i, lax.rem(i + 1, ni), piece_send.at[0]).wait_recv()
        for d in range(1, ni):
            @pl.when(lax.rem(i + d, ni) != 0)
            def _():
                gather_copy(d).start()
        for d in range(1, nb):
            @pl.when(b + d < nb)
            def _():
                column_copy(i, d).start()

    kall[0:BLOCK] = kv[0:BLOCK]
    vall[0:BLOCK] = kv[BLOCK:PAIR]
    for copy in head_loads:
        copy.wait()
    key_pos = lax.broadcasted_iota(jnp.int32, (BLOCK, PAIR), 0)
    query_pos = lax.rem(lax.broadcasted_iota(jnp.int32, (BLOCK, PAIR), 1), BLOCK)
    causal = key_pos <= query_pos
    for n in range(HEADS // 2):
        sl = slice(n * PAIR, (n + 1) * PAIR)
        band_s[0:BLOCK, sl] = jnp.where(causal, nt(kv[0:BLOCK], qs[sl]), NEG)
        band_dp[0:BLOCK, sl] = nt(kv[BLOCK:PAIR], dos[sl])
    for h in range(HEADS):
        sl = slice(h * BLOCK, (h + 1) * BLOCK)
        do_t[:, sl] = jnp.transpose(dos[sl].astype(F32))

    @pl.when(i > 0)
    def _():
        for t in range(1, holders):
            n = lax.rem(i + t, holders)

            @pl.when(n != i)
            def _():
                piece_copy(kv.at[pl.ds(0, piece)], n, lax.rem(i + 1, ni), piece_send.at[0]).wait_recv()
            for d in range(1, nb):
                @pl.when(b + d < nb)
                def _():
                    column_copy(n, d).start()

    if holders < ni:
        @pl.when(i >= holders)
        def _():
            n = lax.rem(i, holders)
            piece_copy(kv.at[pl.ds(0, piece)], n, lax.rem(i + 1, ni), piece_send.at[0]).wait_recv()
            for d in range(1, nb):
                @pl.when(b + d < nb)
                def _():
                    column_copy(n, d).start()

    @pl.when(dev > 0)
    def _():
        band.wait_recv()

    kall[BLOCK:PAIR] = prev[0:BLOCK]
    vall[BLOCK:PAIR] = prev[BLOCK:PAIR]
    listed = [list_ref[0, n] for n in range(NB)]
    prev_live = listed[0] == dev - 1
    for n in range(1, NB):
        prev_live = jnp.logical_or(prev_live, listed[n] == dev - 1)
    prev_live = jnp.logical_and(prev_live, dev > 0)
    factor = SCALE * LOG2E
    prev_bias = jnp.where(prev_live, 0.0, NEG)
    for n in range(HEADS // 2):
        sl = slice(n * PAIR, (n + 1) * PAIR)
        before_s = nt(prev[0:BLOCK], qs[sl])
        band_dp[BLOCK:PAIR, sl] = nt(prev[BLOCK:PAIR], dos[sl])
        own_s = band_s[0:BLOCK, sl]
        top = jnp.maximum(jnp.max(own_s, axis=0, keepdims=True),
                          jnp.max(before_s, axis=0, keepdims=True) + prev_bias) * factor
        own_w = jnp.exp2(own_s * factor - top)
        before_w = jnp.exp2(before_s * factor + (prev_bias - top))
        band_s[0:BLOCK, sl] = own_w
        band_s[BLOCK:PAIR, sl] = before_w
        stat[0:1, sl] = top
        stat[1:2, sl] = jnp.sum(own_w, axis=0, keepdims=True) + jnp.sum(before_w, axis=0, keepdims=True)

    for a in range(nb - 1):
        @pl.when(a < b)
        def _():
            @pl.when(i == 0)
            def _():
                root_column_wait(a).wait_recv()

            @pl.when(i > 0)
            def _():
                for n in range(holders):
                    column_wait(a, n).wait_recv()

    biases = []
    anchor_ids = []
    for e in range(STRIPES):
        block = listed[BAND + e]
        dead = jnp.logical_or(block == dev, jnp.logical_and(block == dev - 1, prev_live))
        for f in range(e):
            dead = jnp.logical_or(dead, block == listed[BAND + f])
        biases.append(jnp.where(dead, NEG, 0.0))
        anchor_ids.append(block // ni)
        at = slice(PAIR + e * BLOCK, PAIR + (e + 1) * BLOCK)
        picked = anch[anchor_ids[e]]
        kall[at] = picked[0:BLOCK]
        vall[at] = picked[BLOCK:PAIR]
    k_t[...] = jnp.transpose(kall[...].astype(F32)).astype(BF16)
    v_t[...] = jnp.transpose(vall[...].astype(F32)).astype(BF16)

    for n in range(HEADS // 2):
        sl = slice(n * PAIR, (n + 1) * PAIR)
        stripe = nt(kall[PAIR:], qs[sl])
        scores = [stripe[e * BLOCK:(e + 1) * BLOCK] for e in range(STRIPES)]
        band_top = stat[0:1, sl]
        peak = band_top
        for bias, block in zip(biases, scores):
            peak = jnp.maximum(peak, (jnp.max(block, axis=0, keepdims=True) + bias) * factor)
        rescale = jnp.exp2(band_top - peak)
        total = stat[1:2, sl] * rescale
        weights = []
        for bias, block in zip(biases, scores):
            weight = jnp.exp2(block * factor + (bias - peak))
            weights.append(weight)
            total = total + jnp.sum(weight, axis=0, keepdims=True)
        inverse = 1.0 / total
        band_inverse = rescale * inverse
        probs = [band_s[0:BLOCK, sl] * band_inverse, band_s[BLOCK:PAIR, sl] * band_inverse]
        probs += [weight * inverse for weight in weights]
        for m in range(NB):
            p_s[m * BLOCK:(m + 1) * BLOCK, sl] = probs[m].astype(BF16)
        out = nn(v_t[...], p_s[:, sl]).astype(BF16).astype(F32)
        o_t[:, sl] = out
        delta = jnp.sum(out * do_t[:, sl], axis=0, keepdims=True)
        stripe_dp = nt(vall[PAIR:], dos[sl])
        grads = [band_dp[0:BLOCK, sl], band_dp[BLOCK:PAIR, sl]]
        grads += [stripe_dp[e * BLOCK:(e + 1) * BLOCK] for e in range(STRIPES)]
        for m in range(NB):
            ds_s[m * BLOCK:(m + 1) * BLOCK, sl] = (probs[m] * (grads[m] - delta)).astype(BF16)

    stripe_gk = nn(ds_s[PAIR:, :], qs[...]) * SCALE
    stripe_gv = nn(p_s[PAIR:, :], dos[...])

    def anchor_sum(grad, a):
        total = None
        for e in range(STRIPES):
            term = grad[e * BLOCK:(e + 1) * BLOCK] * jnp.where(anchor_ids[e] == a, 1.0, 0.0)
            total = term if total is None else total + term
        return total

    def gcol_copy(a):
        return pltpu.make_async_remote_copy(
            src_ref=gsend.at[a], dst_ref=grecv.at[b], send_sem=gcol_send.at[a],
            recv_sem=gcol_recv.at[b], device_id=(a, i), device_id_type=MESH)

    def gcol_wait(d):
        return pltpu.make_async_remote_copy(
            src_ref=gsend.at[0], dst_ref=grecv.at[b + d], send_sem=gcol_send.at[0],
            recv_sem=gcol_recv.at[b + d], device_id=(lax.rem(b + 1, nb), i), device_id_type=MESH)

    for a in range(nb - 1):
        @pl.when(a < b)
        def _():
            gsend[a, 0:BLOCK] = anchor_sum(stripe_gk, a).astype(BF16)
            gsend[a, BLOCK:PAIR] = anchor_sum(stripe_gv, a).astype(BF16)
            gcol_copy(a).start()
    mine[0:BLOCK] = anchor_sum(stripe_gk, b)
    mine[BLOCK:PAIR] = anchor_sum(stripe_gv, b)

    band_gk = nn(ds_s[0:PAIR, :], qs[...]) * SCALE
    band_gv = nn(p_s[0:PAIR, :], dos[...])
    own[0:BLOCK] = band_gk[0:BLOCK]
    own[BLOCK:PAIR] = band_gv[0:BLOCK]
    bsend[0:BLOCK] = band_gk[BLOCK:PAIR].astype(BF16)
    bsend[BLOCK:PAIR] = band_gv[BLOCK:PAIR].astype(BF16)
    before = jnp.maximum(dev - 1, 0)
    back = pltpu.make_async_remote_copy(
        src_ref=bsend, dst_ref=brecv, send_sem=back_sem.at[0], recv_sem=back_sem.at[1],
        device_id=(before // ni, lax.rem(before, ni)), device_id_type=MESH)

    for d in range(1, nb):
        @pl.when(b + d < nb)
        def _():
            gcol_wait(d).wait_recv()
            mine[...] += grecv[b + d].astype(F32)
    psend[...] = mine[...].astype(BF16)

    def gp_copy(d):
        n = lax.rem(i + d, ni)
        return pltpu.make_async_remote_copy(
            src_ref=psend.at[part(n)], dst_ref=precv.at[i], send_sem=gp_send.at[d],
            recv_sem=gp_recv.at[i], device_id=(b, n), device_id_type=MESH)

    def gp_wait(d):
        n = lax.rem(i + d, ni)
        return pltpu.make_async_remote_copy(
            src_ref=psend.at[pl.ds(0, piece)], dst_ref=precv.at[n], send_sem=gp_send.at[0],
            recv_sem=gp_recv.at[n], device_id=(b, n), device_id_type=MESH)

    for d in range(1, ni):
        @pl.when(lax.rem(i + d, ni) < holders)
        def _():
            gp_copy(d).start()

    @pl.when(dev > 0)
    def _():
        back.start()

    def write_heads(heads):
        for h in heads:
            sl = slice(h * BLOCK, (h + 1) * BLOCK)
            gq = nn(k_t[...], ds_s[:, sl]) * SCALE
            gq_ref[:, sl] = jnp.transpose(gq).astype(BF16)
            att_ref[:, sl] = jnp.transpose(o_t[:, sl]).astype(BF16)

    write_heads(range(0, HEADS // 2))

    def top_copy(n):
        return pltpu.make_async_remote_copy(
            src_ref=tsend, dst_ref=trecv.at[n], send_sem=top_send.at[0], recv_sem=top_recv.at[n],
            device_id=(b, 0), device_id_type=MESH)

    def top_wait(n):
        return pltpu.make_async_remote_copy(
            src_ref=tsend, dst_ref=trecv.at[n], send_sem=top_send.at[0], recv_sem=top_recv.at[n],
            device_id=(b, n), device_id_type=MESH)

    @pl.when(i < holders)
    def _():
        total = mine[part(i)]
        for d in range(1, ni):
            gp_wait(d).wait_recv()
            total = total + precv[lax.rem(i + d, ni)].astype(F32)
        total_ref[...] = total
        tsend[...] = total.astype(BF16)

        @pl.when(i > 0)
        def _():
            top_copy(i).start()

    write_heads(range(HEADS // 2, HEADS))

    @pl.when(dev < last)
    def _():
        back.wait_recv()
        own[...] += brecv[...].astype(F32)

    @pl.when(i == 0)
    def _():
        own[0:piece] += total_ref[...]
        for n in range(1, holders):
            top_wait(n).wait_recv()
            own[n * piece:(n + 1) * piece] += trecv[n].astype(F32)

    gk_ref[...] = own[0:BLOCK]
    gv_ref[...] = own[BLOCK:PAIR]

    @pl.when(dev < last)
    def _():
        band.wait_send()

    @pl.when(dev > 0)
    def _():
        back.wait_send()

    @pl.when(i == 0)
    def _():
        for n in range(1, holders):
            scatter_copy(n).wait_send()
        for j in range(1, ni):
            root_copy(j).wait_send()

    @pl.when(holder)
    def _():
        for d in range(1, ni):
            @pl.when(lax.rem(i + d, ni) != 0)
            def _():
                gather_copy(d).wait_send()
        top_copy(i).wait_send()

    for d in range(1, nb):
        @pl.when(b + d < nb)
        def _():
            @pl.when(i == 0)
            def _():
                root_column(d).wait_send()

            @pl.when(i > 0)
            def _():
                for n in range(holders):
                    column_copy(n, d).wait_send()
    for a in range(nb - 1):
        @pl.when(a < b)
        def _():
            gcol_copy(a).wait_send()
    for d in range(1, ni):
        @pl.when(lax.rem(i + d, ni) < holders)
        def _():
            gp_copy(d).wait_send()


def write_out(*refs):
    for n in range(4):
        refs[4 + n][...] = refs[n][...]


def solution(mesh):
    nb, ni = mesh.shape["blk"], mesh.shape["inner"]
    holders = min(ni, 8)
    piece = PAIR // holders
    dma = pltpu.SemaphoreType.DMA

    def shards(queries, keys, values, out_grad, block_list):
        any_spec = pl.BlockSpec(memory_space=pl.ANY)
        vmem_spec = pl.BlockSpec(memory_space=pltpu.VMEM)
        results = pl.pallas_call(
            functools.partial(kernel, nb, ni, holders),
            out_shape=(
                jax.ShapeDtypeStruct((BLOCK, ROWS), BF16),
                jax.ShapeDtypeStruct((BLOCK, ROWS), BF16),
                jax.ShapeDtypeStruct((BLOCK, HEAD_DIM), F32),
                jax.ShapeDtypeStruct((BLOCK, HEAD_DIM), F32),
            ),
            in_specs=[any_spec] * 4 + [pl.BlockSpec(memory_space=pltpu.SMEM)],
            out_specs=(vmem_spec,) * 4,
            scratch_shapes=[
                pltpu.VMEM((ROWS, HEAD_DIM), BF16),
                pltpu.VMEM((ROWS, HEAD_DIM), BF16),
                pltpu.VMEM((PAIR, HEAD_DIM), BF16),
                pltpu.VMEM((PAIR, HEAD_DIM), BF16),
                pltpu.VMEM((nb, PAIR, HEAD_DIM), BF16),
                pltpu.VMEM((HEAD_DIM, ROWS), F32),
                pltpu.VMEM((NB * BLOCK, HEAD_DIM), BF16),
                pltpu.VMEM((NB * BLOCK, HEAD_DIM), BF16),
                pltpu.VMEM((HEAD_DIM, NB * BLOCK), BF16),
                pltpu.VMEM((HEAD_DIM, NB * BLOCK), BF16),
                pltpu.VMEM((PAIR, ROWS), F32),
                pltpu.VMEM((PAIR, ROWS), F32),
                pltpu.VMEM((8, ROWS), F32),
                pltpu.VMEM((NB * BLOCK, ROWS), BF16),
                pltpu.VMEM((NB * BLOCK, ROWS), BF16),
                pltpu.VMEM((HEAD_DIM, ROWS), F32),
                pltpu.VMEM((PAIR, HEAD_DIM), F32),
                pltpu.VMEM((PAIR, HEAD_DIM), F32),
                pltpu.VMEM((nb, PAIR, HEAD_DIM), BF16),
                pltpu.VMEM((nb, PAIR, HEAD_DIM), BF16),
                pltpu.VMEM((PAIR, HEAD_DIM), BF16),
                pltpu.VMEM((ni, piece, HEAD_DIM), BF16),
                pltpu.VMEM((piece, HEAD_DIM), F32),
                pltpu.VMEM((piece, HEAD_DIM), BF16),
                pltpu.VMEM((holders, piece, HEAD_DIM), BF16),
                pltpu.VMEM((PAIR, HEAD_DIM), BF16),
                pltpu.VMEM((PAIR, HEAD_DIM), BF16),
                dma((2,)),
                dma((2 * HEADS,)),
                dma((2,)),
                dma((holders,)),
                dma((ni,)),
                dma((holders,)),
                dma((nb, holders)),
                dma((nb, holders)),
                dma((2,)),
                dma((nb,)),
                dma((nb,)),
                dma((ni,)),
                dma((ni,)),
                dma((1,)),
                dma((holders,)),
            ],
            compiler_params=pltpu.CompilerParams(
                collective_id=0, has_side_effects=True, vmem_limit_bytes=60 * 1024 * 1024
            ),
            name="sparse_attention",
        )(queries, keys, values, out_grad, block_list)
        return pl.pallas_call(
            write_out,
            out_shape=tuple(jax.ShapeDtypeStruct(r.shape, r.dtype) for r in results),
            in_specs=[vmem_spec] * 4,
            out_specs=(vmem_spec,) * 4,
            name="write_out",
        )(*results)

    spec = P(("blk", "inner"), None)
    return jax.shard_map(
        shards, mesh=mesh, in_specs=(spec,) * 5, out_specs=(spec,) * 4, check_vma=False
    )
```
